32 devices in a mesh: vocab: 8 (over y, x, core), width: 4 (over z).
Axes of the slice: x: 2, y: 2, z: 4, core: 2. Of those that a mesh axis runs over, the one named last changes fastest.
Arguments:
- hidden: bfloat16 [256, 2880], P('width'), may hold values from -60 to 60
- gain: float32 [2880], replicated, may hold values from 0.1 to 1.9
- unembed: bfloat16 [2880, 50176], P('width', 'vocab'), may hold values from -8 to 8
- targets: int32 [256], replicated, may hold values from 0 to 50175
- seq_ids: int32 [256], replicated, may hold values from 0 to 47, as said below
Outputs:
- log_normalizer: float32 [256], P('width')
- entropy: float32 [256], P('width')
- token_logprob: float32 [256], P('width')
- seq_mean: float32 [48], replicated
The draws below stay inside these ranges and needn't reach their ends.
Inputs may be any that keep to these rules, and one draw needn't show every extreme that they name: `seq_ids`: rows of one sequence are consecutive and ids never fall; every sequence has at least one row.
All inputs are finite; a program needn't handle non-finite values.
Results may differ from the reference program's by a relative error of at most 0.0014.
Values may be sent and summed in bfloat16 or wider, within the bound.
A program may use at most 128 MiB of HBM per device.

```python
import jax
import jax.numpy as jnp
from jax import lax

D = 2880
ROWS_DEV = 64
SEQS = 48
ROWS = 256
VOCAB = 50176


def pattern_vector(key):
    return jax.random.truncated_normal(jax.random.fold_in(key, 71), -3.0, 3.0, (D,), jnp.float32)


def column_at(key):
    return jax.random.randint(jax.random.fold_in(key, 72), (), 0, VOCAB - 1)


def draw_unembed(key, part):
    weights = jax.random.truncated_normal(jax.random.fold_in(key, 3), -6.0, 6.0, (D, VOCAB), jnp.float32) * 0.056
    amplitude = 260.0
    pattern = pattern_vector(key) * (amplitude / D)
    paired = jnp.stack([pattern, pattern * 0.99], axis=1)
    weights = lax.dynamic_update_slice(weights, paired, (jnp.int32(0), column_at(key).astype(jnp.int32)))
    return weights.astype(jnp.bfloat16)


def draw_hidden(key, part):
    base = jax.random.truncated_normal(jax.random.fold_in(key, 5), -6.0, 6.0, (ROWS, D), jnp.float32)
    scales = jnp.exp(jax.random.uniform(jax.random.fold_in(key, 6), (ROWS, 1), jnp.float32, 0.0, 2.3))
    result = base * scales
    pattern = pattern_vector(key)
    row_ids = jnp.arange(ROWS)
    strength = jnp.where(row_ids % 8 == 3, 1.0, jnp.where(row_ids % 8 == 6, 0.85, jnp.where(row_ids % 8 == 1, 0.6, 0.0)))[:, None]
    result = strength * pattern[None, :] * scales + (1.0 - strength) * result
    return result.astype(jnp.bfloat16)


def draw_seq_ids(key, part):
    order = jax.random.permutation(jax.random.fold_in(key, 91), ROWS - 1)
    cuts = order[:SEQS - 1].astype(jnp.int32) + 1
    row_ids = jnp.arange(ROWS, dtype=jnp.int32)
    return jnp.sum((cuts[None, :] <= row_ids[:, None]).astype(jnp.int32), axis=1).astype(jnp.int32)


def plant(entries, stream_key, low, largest):
    place = [jax.random.randint(jax.random.fold_in(stream_key, axis), (), 0, length) for axis, length in enumerate(entries.shape)]
    main_axis = entries.shape.index(max(entries.shape))
    beside = place[:main_axis] + [(place[main_axis] + 1) % entries.shape[main_axis]] + place[main_axis + 1:]
    return entries.at[tuple(place)].set(low).at[tuple(beside)].set(largest)


def setup_inputs(seed: int = 0) -> dict:
    seeds = jax.random.split(jax.random.key(seed), 6)
    return {
        "hidden": draw_hidden(jax.random.fold_in(seeds[5], 71), 0),
        "gain": jnp.clip(1.0 + 0.18 * jax.random.normal(seeds[1], (D,), jnp.float32), 0.1, 1.9),
        "unembed": draw_unembed(jax.random.fold_in(seeds[5], 71), 0),
        "targets": plant(jax.random.randint(seeds[3], (ROWS,), 0, VOCAB), jax.random.fold_in(seeds[3], 1), 0, VOCAB - 1).astype(jnp.int32),
        "seq_ids": draw_seq_ids(jax.random.fold_in(seeds[5], 71), 0),
    }


def reference(hidden, gain, unembed, targets, seq_ids):
    values = hidden.astype(jnp.float32)
    square = lax.optimization_barrier(jnp.mean(values * values, axis=1, keepdims=True))
    normed = (values * lax.rsqrt(square + 1e-05) * gain[None, :]).astype(jnp.bfloat16)
    blocks = ROWS // ROWS_DEV
    normed_blocks = normed.reshape(blocks, ROWS_DEV, D)
    target_blocks = targets.astype(jnp.int32).reshape(blocks, ROWS_DEV)

    def row_block(inputs):
        block_rows, block_targets = inputs
        logits = jnp.dot(block_rows, unembed, preferred_element_type=jnp.float32)
        row_max = lax.optimization_barrier(jnp.max(logits, axis=1))
        shifted = jnp.exp(logits - row_max[:, None])
        exp_total = lax.optimization_barrier(jnp.sum(shifted, axis=1))
        log_norm = row_max + jnp.log(exp_total)
        row_entropy = log_norm - lax.optimization_barrier(jnp.sum(shifted * logits, axis=1)) / exp_total
        target_logit = jnp.take_along_axis(logits, block_targets[:, None], axis=1)[:, 0]
        return (log_norm, row_entropy, target_logit - log_norm)
    log_normalizer, entropy, token_logprob = lax.map(row_block, (normed_blocks, target_blocks))
    log_normalizer = log_normalizer.reshape(ROWS)
    entropy = entropy.reshape(ROWS)
    token_logprob = token_logprob.reshape(ROWS)
    member = (seq_ids[:, None] == jnp.arange(SEQS, dtype=jnp.int32)[None, :]).astype(jnp.float32)
    seq_sums = jnp.dot(token_logprob, member, precision=lax.Precision.HIGHEST)
    seq_counts = lax.optimization_barrier(jnp.sum(member, axis=0))
    return (log_normalizer, entropy, token_logprob, seq_sums / seq_counts)
```

```python
import jax
import jax.numpy as jnp
from jax import lax
from jax.sharding import PartitionSpec as P

SEQS = 48


def merged(part, axis, combine):
    gathered = jax.tree.map(lambda a: lax.all_gather(a, axis), part)

    def take(source):
        return jax.tree.map(lambda a: lax.dynamic_index_in_dim(a, source, 0, False), gathered)

    return lax.fori_loop(
        1, lax.axis_size(axis), lambda source, state: combine(state, take(source)), take(0)
    )


def combine_parts(first_part, second_part):
    merged_max = jnp.maximum(first_part[0], second_part[0])
    left_scale = jnp.exp(first_part[0] - merged_max)
    right_scale = jnp.exp(second_part[0] - merged_max)
    return (
        merged_max,
        first_part[1] * left_scale + second_part[1] * right_scale,
        first_part[2] * left_scale + second_part[2] * right_scale,
        first_part[3] + second_part[3],
    )


def local_stats(logits, wanted, first_col):
    column = first_col + lax.broadcasted_iota(jnp.int32, logits.shape, 1)
    target_hit = jnp.sum(jnp.where(column == wanted[:, None], logits, 0.0), axis=1)
    local_max = jnp.max(logits, axis=1)
    shifted = jnp.exp(logits - local_max[:, None])
    return (local_max, jnp.sum(shifted, axis=1), jnp.sum(shifted * logits, axis=1), target_hit)


def local(hidden, gain, unembed, targets, seq_ids):
    widths = lax.axis_size("width")
    owner = lax.axis_index("width")
    own_rows = hidden.shape[0]
    values = hidden.astype(jnp.float32)
    square = jnp.mean(values * values, axis=1, keepdims=True)
    normed = (values * lax.rsqrt(square + 1e-05) * gain[None, :]).astype(jnp.bfloat16)
    own_features = lax.all_to_all(normed, "width", split_axis=1, concat_axis=0, tiled=True)
    partial = jnp.dot(own_features, unembed, preferred_element_type=jnp.float32)
    logits = lax.psum_scatter(partial, "width", scatter_dimension=1, tiled=True)
    col_share = logits.shape[1]
    first_col = (lax.axis_index("vocab") * widths + owner) * col_share
    stats = local_stats(logits, targets, first_col)
    all_max, all_total, all_weighted, all_target = merged(stats, ("vocab", "width"), combine_parts)
    row_start = owner * own_rows
    row_max = lax.dynamic_slice_in_dim(all_max, row_start, own_rows, 0)
    exp_total = lax.dynamic_slice_in_dim(all_total, row_start, own_rows, 0)
    weighted = lax.dynamic_slice_in_dim(all_weighted, row_start, own_rows, 0)
    target_logit = lax.dynamic_slice_in_dim(all_target, row_start, own_rows, 0)
    log_normalizer = row_max + jnp.log(exp_total)
    entropy = log_normalizer - weighted / exp_total
    token_logprob = target_logit - log_normalizer
    own_seq = lax.dynamic_slice_in_dim(seq_ids, owner * own_rows, own_rows, 0)
    member = (own_seq[:, None] == jnp.arange(SEQS, dtype=jnp.int32)[None, :]).astype(jnp.float32)
    seq_sums, seq_counts = lax.psum(
        (jnp.dot(token_logprob, member, precision=lax.Precision.HIGHEST), jnp.sum(member, axis=0)),
        "width",
    )
    return (log_normalizer, entropy, token_logprob, seq_sums / seq_counts)


def solution(mesh):
    placed = (P("width", None), P(), P("width", "vocab"), P(), P())
    return jax.shard_map(
        local,
        mesh=mesh,
        in_specs=placed,
        out_specs=(P("width"), P("width"), P("width"), P()),
        check_vma=False,
    )
```

```python
import functools

import jax
import jax.numpy as jnp
from jax import lax
from jax.experimental import pallas as pl
from jax.experimental.pallas import tpu as pltpu
from jax.sharding import PartitionSpec as P

SEQS = 48
LANES = 128
LAG = 3
LOWEST = -1e38
MESH = pl.DeviceIdType.MESH


def kernel(
    n, nv, hidden_ref, gain_ref, unembed_ref, targets_ref, seq_ref, out_ref,
    weights, blocks, rows_in, buf, target_cols, state, packed, gathered, final,
    w_sem, own_sem, x_send, x_recv, c_send, c_recv, v_send, v_recv, f_send, f_recv,
):
    me = lax.axis_index("width")
    my_vocab = lax.axis_index("vocab")
    own_rows, width_dim = hidden_ref.shape
    share = width_dim // n
    half = (n // 2) * own_rows
    chunks = unembed_ref.shape[1] // LANES
    last = n - 1

    load_weights = pltpu.make_async_copy(unembed_ref, weights, w_sem)
    load_weights.start()

    barrier = pltpu.get_barrier_semaphore()
    for k in range(1, n):
        pl.semaphore_signal(
            barrier, inc=1, device_id={"width": lax.rem(me + k, n)}, device_id_type=MESH
        )
    for k in range(1, nv):
        pl.semaphore_signal(
            barrier, inc=1, device_id={"vocab": lax.rem(my_vocab + k, nv)}, device_id_type=MESH
        )

    values = hidden_ref[...].astype(jnp.float32)
    square = jnp.mean(values * values, axis=1, keepdims=True)
    normed = (values * lax.rsqrt(square + 1e-05) * gain_ref[...]).astype(jnp.bfloat16)
    for j in range(n):
        blocks[j] = normed[:, j * share : (j + 1) * share]

    pl.semaphore_wait(barrier, n - 1 + nv - 1)

    def row_copy(peer, source):
        return pltpu.make_async_remote_copy(
            src_ref=blocks.at[peer],
            dst_ref=rows_in.at[source],
            send_sem=x_send.at[peer],
            recv_sem=x_recv.at[source],
            device_id={"width": peer},
            device_id_type=MESH,
        )

    for k in range(1, n):
        row_copy(lax.rem(me + k, n), me).start()
    own = pltpu.make_async_copy(blocks.at[me], rows_in.at[me], own_sem)
    own.start()

    target_row = targets_ref[...].astype(jnp.float32)
    target_all = jnp.transpose(jnp.broadcast_to(target_row, (LANES, 2 * half)))
    target_cols[0] = target_all[:half]
    target_cols[1] = target_all[half:]
    state[0] = jnp.full((half, LANES), LOWEST, jnp.float32)
    for k in range(1, 4):
        state[k] = jnp.zeros((half, LANES), jnp.float32)

    own.wait()
    load_weights.wait()
    for k in range(1, n):
        peer = lax.rem(me + k, n)
        row_copy(peer, peer).wait_recv()

    def chunk_copy(side, c, peer):
        return pltpu.make_async_remote_copy(
            src_ref=buf.at[side, c],
            dst_ref=buf.at[side, c],
            send_sem=c_send.at[side, c],
            recv_sem=c_recv.at[side, c],
            device_id={"width": peer},
            device_id_type=MESH,
        )

    first_col = my_vocab * (chunks * LANES)
    lane = lax.broadcasted_iota(jnp.int32, (half, LANES), 1)

    def partial_logits(side, c):
        cols = pl.ds(pl.multiple_of(c * LANES, LANES), LANES)
        x = rows_in[side * (n // 2) : (side + 1) * (n // 2)].reshape(half, share)
        return jnp.dot(x, weights[:, cols], preferred_element_type=jnp.float32)

    def take_stats(side, c, logits):
        column = (first_col + c * LANES + lane).astype(jnp.float32)
        old_max = state[0]
        new_max = jnp.maximum(old_max, logits)
        scale = jnp.exp(old_max - new_max)
        shifted = jnp.exp(logits - new_max)
        state[0] = new_max
        state[1] = state[1] * scale + shifted
        state[2] = state[2] * scale + shifted * logits
        state[3] = state[3] + jnp.where(column == target_cols[side], logits, 0.0)

    def advance(side, c, head, tail, peer):
        @pl.when((c >= 0) & (c < chunks))
        def _():
            mine = partial_logits(side, c)

            @pl.when(me == head)
            def _():
                buf[side, c] = mine
                chunk_copy(side, c, peer).start()

            @pl.when(me != head)
            def _():
                chunk_copy(side, c, peer).wait_recv()
                total = buf[side, c] + mine

                @pl.when(me != tail)
                def _():
                    buf[side, c] = total
                    chunk_copy(side, c, peer).start()

                @pl.when(me == tail)
                def _():
                    take_stats(side, c, total)

    down = lax.rem(me + n - 1, n)
    up = lax.rem(me + 1, n)

    def step(s, carry):
        advance(0, s - (last - me) * LAG, last, 0, down)
        advance(1, s - me * LAG, 0, last, up)
        return carry

    lax.fori_loop(0, chunks + last * LAG, step, 0)

    def stats_copy(peer, source):
        return pltpu.make_async_remote_copy(
            src_ref=packed.at[0],
            dst_ref=gathered.at[source],
            send_sem=v_send.at[peer],
            recv_sem=v_recv.at[source],
            device_id={"vocab": peer},
            device_id_type=MESH,
        )

    def final_copy(side, peer):
        return pltpu.make_async_remote_copy(
            src_ref=packed.at[1],
            dst_ref=final.at[side],
            send_sem=f_send.at[peer],
            recv_sem=f_recv.at[side],
            device_id={"width": peer},
            device_id_type=MESH,
        )

    def finish(side):
        lane_max = state[0]
        row_max = jnp.max(lane_max, axis=1, keepdims=True)
        scale = jnp.exp(lane_max - row_max)
        columns = (
            row_max,
            jnp.sum(state[1] * scale, axis=1, keepdims=True),
            jnp.sum(state[2] * scale, axis=1, keepdims=True),
            jnp.sum(state[3], axis=1, keepdims=True),
        )
        wide = jnp.zeros((half, LANES), jnp.float32)
        for k in range(4):
            wide = jnp.where(lane == k, columns[k], wide)
        flat = jnp.transpose(wide)[:8]
        packed[0] = flat
        for k in range(1, nv):
            stats_copy(lax.rem(my_vocab + k, nv), my_vocab).start()
        gathered[my_vocab] = flat
        for k in range(1, nv):
            peer = lax.rem(my_vocab + k, nv)
            stats_copy(peer, peer).wait_recv()
        parts = [gathered[v] for v in range(nv)]
        top = functools.reduce(jnp.maximum, [part[0:1] for part in parts])
        total = jnp.zeros_like(top)
        weighted = jnp.zeros_like(top)
        target = jnp.zeros_like(top)
        for part in parts:
            factor = jnp.exp(part[0:1] - top)
            total = total + part[1:2] * factor
            weighted = weighted + part[2:3] * factor
            target = target + part[3:4]
        log_normalizer = top + jnp.log(total)
        rows = lax.broadcasted_iota(jnp.int32, (8, half), 0)
        result = jnp.where(
            rows == 0,
            log_normalizer,
            jnp.where(rows == 1, log_normalizer - weighted / total, target - log_normalizer),
        )
        packed[1] = result
        for k in range(1, n):
            final_copy(side, lax.rem(me + k, n)).start()
        final[side] = result

    @pl.when(me == 0)
    def _():
        finish(0)

    @pl.when(me == last)
    def _():
        finish(1)

    @pl.when(me != 0)
    def _():
        final_copy(0, 0).wait_recv()

    @pl.when(me != last)
    def _():
        final_copy(1, 0).wait_recv()

    ids = lax.broadcasted_iota(jnp.int32, (LANES, half), 0)
    sums = jnp.zeros((LANES, 1), jnp.float32)
    counts = jnp.zeros((LANES, 1), jnp.float32)
    for side in range(2):
        member = ids == seq_ref[:, side * half : (side + 1) * half]
        sums = sums + jnp.sum(jnp.where(member, final[side, 2:3], 0.0), axis=1, keepdims=True)
        counts = counts + jnp.sum(member.astype(jnp.float32), axis=1, keepdims=True)
    means = sums / jnp.maximum(counts, 1.0)
    out_ref[...] = jnp.zeros_like(out_ref)
    out_ref[3:4, :] = jnp.transpose(jnp.broadcast_to(means, (LANES, LANES)))[0:1]
    for w in range(n):

        @pl.when(me == w)
        def _():
            start = (w % (n // 2)) * own_rows
            out_ref[0:3, 0:own_rows] = final[w // (n // 2), 0:3, start : start + own_rows]

    for k in range(1, n):
        row_copy(lax.rem(me + k, n), me).wait_send()

    def drain(c, carry):
        @pl.when(me != 0)
        def _():
            chunk_copy(0, c, down).wait_send()

        @pl.when(me != last)
        def _():
            chunk_copy(1, c, up).wait_send()

        return carry

    lax.fori_loop(0, chunks, drain, 0)

    @pl.when((me == 0) | (me == last))
    def _():
        for k in range(1, nv):
            stats_copy(lax.rem(my_vocab + k, nv), my_vocab).wait_send()
        for k in range(1, n):
            final_copy(0, lax.rem(me + k, n)).wait_send()


def solution(mesh):
    n, nv = mesh.shape["width"], mesh.shape["vocab"]

    def local(hidden, gain, unembed, targets, seq_ids):
        own_rows, width_dim = hidden.shape
        share, columns = unembed.shape
        half = (n // 2) * own_rows
        chunks = columns // LANES
        vmem = pl.BlockSpec(memory_space=pltpu.VMEM)
        out = pl.pallas_call(
            functools.partial(kernel, n, nv),
            out_shape=jax.ShapeDtypeStruct((8, LANES), jnp.float32),
            in_specs=[vmem, vmem, pl.BlockSpec(memory_space=pl.ANY), vmem, vmem],
            out_specs=vmem,
            scratch_shapes=[
                pltpu.VMEM((share, columns), jnp.bfloat16),
                pltpu.VMEM((n, own_rows, share), jnp.bfloat16),
                pltpu.VMEM((n, own_rows, share), jnp.bfloat16),
                pltpu.VMEM((2, chunks, half, LANES), jnp.float32),
                pltpu.VMEM((2, half, LANES), jnp.float32),
                pltpu.VMEM((4, half, LANES), jnp.float32),
                pltpu.VMEM((2, 8, half), jnp.float32),
                pltpu.VMEM((nv, 8, half), jnp.float32),
                pltpu.VMEM((2, 8, half), jnp.float32),
                pltpu.SemaphoreType.DMA,
                pltpu.SemaphoreType.DMA,
                pltpu.SemaphoreType.DMA((n,)),
                pltpu.SemaphoreType.DMA((n,)),
                pltpu.SemaphoreType.DMA((2, chunks)),
                pltpu.SemaphoreType.DMA((2, chunks)),
                pltpu.SemaphoreType.DMA((nv,)),
                pltpu.SemaphoreType.DMA((nv,)),
                pltpu.SemaphoreType.DMA((n,)),
                pltpu.SemaphoreType.DMA((2,)),
            ],
            compiler_params=pltpu.CompilerParams(
                collective_id=0, has_side_effects=True, vmem_limit_bytes=66_000_000
            ),
        )(hidden, gain[None, :], unembed, targets[None, :], seq_ids[None, :])
        return out[0, :own_rows], out[1, :own_rows], out[2, :own_rows], out[3, :SEQS]

    return jax.shard_map(
        local,
        mesh=mesh,
        in_specs=(P("width", None), P(), P("width", "vocab"), P(), P()),
        out_specs=(P("width"), P("width"), P("width"), P()),
        check_vma=False,
    )
```

```python
import functools

import jax
import jax.numpy as jnp
from jax import lax
from jax.experimental import pallas as pl
from jax.experimental.pallas import tpu as pltpu
from jax.sharding import PartitionSpec as P

SEQS = 48
LANES = 128
LAG = 5
GROUPS = 2
LOWEST = -1e38
MESH = pl.DeviceIdType.MESH


def send_order(me, n):
    sign = jnp.where(me < n // 2, -1, 1)
    return [lax.rem(me + sign * k + n, n) for k in range(1, n)]


def kernel(
    n, nv, hidden_ref, gain_ref, unembed_ref, targets_ref, seq_ref, out_ref,
    weights, blocks, rows_in, buf, target_cols, state, packed, gathered, final,
    w_sem, own_sem, x_send, x_recv, c_send, c_recv, v_send, v_recv, f_send, f_recv,
):
    me = lax.axis_index("width")
    my_vocab = lax.axis_index("vocab")
    own_rows, width_dim = hidden_ref.shape
    share = width_dim // n
    half = (n // 2) * own_rows
    chunks = unembed_ref.shape[1] // LANES
    last = n - 1
    group_blocks = n // 2 // GROUPS
    group_rows = group_blocks * own_rows
    items = GROUPS * chunks
    slots = last * LAG + 1

    early = chunks // 7 * LANES
    loads = []
    for k, cols in enumerate((pl.ds(0, early), pl.ds(early, chunks * LANES - early))):
        loads.append(
            pltpu.make_async_copy(unembed_ref.at[:, cols], weights.at[:, cols], w_sem.at[k])
        )
        loads[k].start()

    barrier = pltpu.get_barrier_semaphore()
    for k in range(1, n):
        pl.semaphore_signal(
            barrier, inc=1, device_id={"width": lax.rem(me + k, n)}, device_id_type=MESH
        )
    for k in range(1, nv):
        pl.semaphore_signal(
            barrier, inc=1, device_id={"vocab": lax.rem(my_vocab + k, nv)}, device_id_type=MESH
        )

    values = hidden_ref[...].astype(jnp.float32)
    square = jnp.mean(values * values, axis=1, keepdims=True)
    normed = (values * lax.rsqrt(square + 1e-05) * gain_ref[...][None, :]).astype(jnp.bfloat16)
    for j in range(n):
        blocks[j] = normed[:, j * share : (j + 1) * share]

    pl.semaphore_wait(barrier, n - 1 + nv - 1)

    def row_copy(peer, source):
        return pltpu.make_async_remote_copy(
            src_ref=blocks.at[peer],
            dst_ref=rows_in.at[source],
            send_sem=x_send.at[peer],
            recv_sem=x_recv.at[source],
            device_id={"width": peer},
            device_id_type=MESH,
        )

    for peer in send_order(me, n):
        row_copy(peer, me).start()
    own = pltpu.make_async_copy(blocks.at[me], rows_in.at[me], own_sem)
    own.start()

    target_row = targets_ref[...].astype(jnp.float32)
    target_all = jnp.transpose(jnp.broadcast_to(target_row, (LANES, 2 * half)))
    target_cols[0] = target_all[:half]
    target_cols[1] = target_all[half:]
    state[0] = jnp.full((half, LANES), LOWEST, jnp.float32)
    for k in range(1, 4):
        state[k] = jnp.zeros((half, LANES), jnp.float32)

    own.wait()
    loads[0].wait()

    def chunk_copy(side, c, peer):
        return pltpu.make_async_remote_copy(
            src_ref=buf.at[side, c],
            dst_ref=buf.at[side, c],
            send_sem=c_send.at[side, lax.rem(c, slots)],
            recv_sem=c_recv.at[side, lax.rem(c, slots)],
            device_id={"width": peer},
            device_id_type=MESH,
        )

    first_col = my_vocab * (chunks * LANES)
    lane = lax.broadcasted_iota(jnp.int32, (half, LANES), 1)
    item_lane = lax.broadcasted_iota(jnp.int32, (group_rows, LANES), 1)

    def partial_logits(first_block, c):
        cols = pl.ds(pl.multiple_of(c * LANES, LANES), LANES)
        x = rows_in[pl.ds(first_block, group_blocks)].reshape(group_rows, share)
        return jnp.dot(x, weights[:, cols], preferred_element_type=jnp.float32)

    def take_stats(side, first_block, c, logits):
        rows = pl.ds(pl.multiple_of((first_block - side * (n // 2)) * own_rows, 8), group_rows)
        column = (first_col + c * LANES + item_lane).astype(jnp.float32)
        old_max = state[0, rows]
        new_max = jnp.maximum(old_max, logits)
        scale = jnp.exp(old_max - new_max)
        shifted = jnp.exp(logits - new_max)
        state[0, rows] = new_max
        state[1, rows] = state[1, rows] * scale + shifted
        state[2, rows] = state[2, rows] * scale + shifted * logits
        state[3, rows] = state[3, rows] + jnp.where(column == target_cols[side, rows], logits, 0.0)

    def advance(side, item, head, tail, peer):
        @pl.when((item >= 0) & (item < items))
        def _():
            group = item // chunks
            c = item - group * chunks
            first_block = group * group_blocks if side == 0 else n - (group + 1) * group_blocks
            for g in range(GROUPS):
                start = g * group_blocks if side == 0 else n - (g + 1) * group_blocks

                @pl.when(item == g * chunks)
                def _():
                    for w in range(start, start + group_blocks):

                        @pl.when(me != w)
                        def _():
                            row_copy(w, w).wait_recv()

            mine = partial_logits(first_block, c)

            @pl.when((me != tail) & (item >= slots))
            def _():
                chunk_copy(side, item - slots, peer).wait_send()

            @pl.when(me == head)
            def _():
                buf[side, item] = mine
                chunk_copy(side, item, peer).start()

            @pl.when(me != head)
            def _():
                chunk_copy(side, item, peer).wait_recv()
                total = buf[side, item] + mine

                @pl.when(me != tail)
                def _():
                    buf[side, item] = total
                    chunk_copy(side, item, peer).start()

                @pl.when(me == tail)
                def _():
                    take_stats(side, first_block, c, total)

    down = lax.rem(me + n - 1, n)
    up = lax.rem(me + 1, n)

    def step(s, carry):
        @pl.when(s == 1)
        def _():
            loads[1].wait()

        advance(0, s - me * LAG, 0, last, up)
        advance(1, s - (last - me) * LAG, last, 0, down)
        return carry

    lax.fori_loop(0, items + last * LAG, step, 0)

    def stats_copy(peer, source):
        return pltpu.make_async_remote_copy(
            src_ref=packed.at[0],
            dst_ref=gathered.at[source],
            send_sem=v_send.at[peer],
            recv_sem=v_recv.at[source],
            device_id={"vocab": peer},
            device_id_type=MESH,
        )

    def final_copy(side, peer):
        return pltpu.make_async_remote_copy(
            src_ref=packed.at[1],
            dst_ref=final.at[side],
            send_sem=f_send.at[peer],
            recv_sem=f_recv.at[side],
            device_id={"width": peer},
            device_id_type=MESH,
        )

    def finish(side):
        lane_max = state[0]
        row_max = jnp.max(lane_max, axis=1, keepdims=True)
        scale = jnp.exp(lane_max - row_max)
        columns = (
            row_max,
            jnp.sum(state[1] * scale, axis=1, keepdims=True),
            jnp.sum(state[2] * scale, axis=1, keepdims=True),
            jnp.sum(state[3], axis=1, keepdims=True),
        )
        wide = jnp.zeros((half, LANES), jnp.float32)
        for k in range(4):
            wide = jnp.where(lane == k, columns[k], wide)
        flat = jnp.transpose(wide)[:8]
        packed[0] = flat
        for k in range(1, nv):
            stats_copy(lax.rem(my_vocab + k, nv), my_vocab).start()
        gathered[my_vocab] = flat
        for k in range(1, nv):
            peer = lax.rem(my_vocab + k, nv)
            stats_copy(peer, peer).wait_recv()
        parts = [gathered[v] for v in range(nv)]
        top = functools.reduce(jnp.maximum, [part[0:1] for part in parts])
        total = jnp.zeros_like(top)
        weighted = jnp.zeros_like(top)
        target = jnp.zeros_like(top)
        for part in parts:
            factor = jnp.exp(part[0:1] - top)
            total = total + part[1:2] * factor
            weighted = weighted + part[2:3] * factor
            target = target + part[3:4]
        log_normalizer = top + jnp.log(total)
        rows = lax.broadcasted_iota(jnp.int32, (8, half), 0)
        result = jnp.where(
            rows == 0,
            log_normalizer,
            jnp.where(rows == 1, log_normalizer - weighted / total, target - log_normalizer),
        )
        packed[1] = result
        for k in range(1, n):
            final_copy(side, lax.rem(me + k, n)).start()
        final[side] = result

    @pl.when(me == last)
    def _():
        finish(0)

    @pl.when(me == 0)
    def _():
        finish(1)

    @pl.when(me != last)
    def _():
        final_copy(0, 0).wait_recv()

    @pl.when(me != 0)
    def _():
        final_copy(1, 0).wait_recv()

    ids = lax.broadcasted_iota(jnp.int32, (LANES, half), 0)
    sums = jnp.zeros((LANES, 1), jnp.float32)
    counts = jnp.zeros((LANES, 1), jnp.float32)
    for side in range(2):
        member = ids == seq_ref[:, side * half : (side + 1) * half]
        sums = sums + jnp.sum(jnp.where(member, final[side, 2:3], 0.0), axis=1, keepdims=True)
        counts = counts + jnp.sum(member.astype(jnp.float32), axis=1, keepdims=True)
    means = sums / jnp.maximum(counts, 1.0)
    out_ref[...] = jnp.zeros_like(out_ref)
    out_ref[3:4, :] = jnp.transpose(jnp.broadcast_to(means, (LANES, LANES)))[0:1]
    for w in range(n):

        @pl.when(me == w)
        def _():
            start = (w % (n // 2)) * own_rows
            out_ref[0:3, 0:own_rows] = final[w // (n // 2), 0:3, start : start + own_rows]

    for k in range(1, n):
        row_copy(lax.rem(me + k, n), me).wait_send()

    def drain(c, carry):
        @pl.when(me != last)
        def _():
            chunk_copy(0, c, up).wait_send()

        @pl.when(me != 0)
        def _():
            chunk_copy(1, c, down).wait_send()

        return carry

    lax.fori_loop(max(items - slots, 0), items, drain, 0)

    @pl.when((me == 0) | (me == last))
    def _():
        for k in range(1, nv):
            stats_copy(lax.rem(my_vocab + k, nv), my_vocab).wait_send()
        for k in range(1, n):
            final_copy(0, lax.rem(me + k, n)).wait_send()


def solution(mesh):
    n, nv = mesh.shape["width"], mesh.shape["vocab"]

    def local(hidden, gain, unembed, targets, seq_ids):
        own_rows, width_dim = hidden.shape
        share, columns = unembed.shape
        half = (n // 2) * own_rows
        items = GROUPS * (columns // LANES)
        vmem = pl.BlockSpec(memory_space=pltpu.VMEM)
        out = pl.pallas_call(
            functools.partial(kernel, n, nv),
            out_shape=jax.ShapeDtypeStruct((8, LANES), jnp.float32),
            in_specs=[vmem, vmem, pl.BlockSpec(memory_space=pl.ANY), vmem, vmem],
            out_specs=vmem,
            scratch_shapes=[
                pltpu.VMEM((share, columns), jnp.bfloat16),
                pltpu.VMEM((n, own_rows, share), jnp.bfloat16),
                pltpu.VMEM((n, own_rows, share), jnp.bfloat16),
                pltpu.VMEM((2, items, half // GROUPS, LANES), jnp.float32),
                pltpu.VMEM((2, half, LANES), jnp.float32),
                pltpu.VMEM((4, half, LANES), jnp.float32),
                pltpu.VMEM((2, 8, half), jnp.float32),
                pltpu.VMEM((nv, 8, half), jnp.float32),
                pltpu.VMEM((2, 8, half), jnp.float32),
                pltpu.SemaphoreType.DMA((2,)),
                pltpu.SemaphoreType.DMA,
                pltpu.SemaphoreType.DMA((n,)),
                pltpu.SemaphoreType.DMA((n,)),
                pltpu.SemaphoreType.DMA((2, (n - 1) * LAG + 1)),
                pltpu.SemaphoreType.DMA((2, (n - 1) * LAG + 1)),
                pltpu.SemaphoreType.DMA((nv,)),
                pltpu.SemaphoreType.DMA((nv,)),
                pltpu.SemaphoreType.DMA((n,)),
                pltpu.SemaphoreType.DMA((2,)),
            ],
            compiler_params=pltpu.CompilerParams(
                collective_id=0, has_side_effects=True, vmem_limit_bytes=66_000_000
            ),
        )(hidden, gain, unembed, targets[None, :], seq_ids[None, :])
        return out[0, :own_rows], out[1, :own_rows], out[2, :own_rows], out[3, :SEQS]

    return jax.shard_map(
        local,
        mesh=mesh,
        in_specs=(P("width", None), P(), P("width", "vocab"), P(), P()),
        out_specs=(P("width"), P("width"), P("width"), P()),
        check_vma=False,
    )
```

```python
import functools

import jax
import jax.numpy as jnp
from jax import lax
from jax.experimental import pallas as pl
from jax.experimental.pallas import tpu as pltpu
from jax.sharding import PartitionSpec as P

SEQS = 48
LANES = 128
LAG = 5
GROUPS = 2
LOWEST = -1e38
MESH = pl.DeviceIdType.MESH


def kernel(
    n, nv, hidden_ref, gain_ref, unembed_ref, targets_ref, seq_ref, out_ref,
    weights, blocks, rows_in, buf, target_cols, state, packed, gathered, final,
    w_sem, own_sem, x_send, x_recv, p_send, p_recv, c_send, c_recv, v_send, v_recv, f_send, f_recv,
):
    me = lax.axis_index("width")
    my_vocab = lax.axis_index("vocab")
    own_rows, width_dim = hidden_ref.shape
    share = width_dim // n
    half = (n // 2) * own_rows
    chunks = unembed_ref.shape[1] // LANES
    last = n - 1
    group_blocks = n // 2 // GROUPS
    group_rows = group_blocks * own_rows
    items = GROUPS * chunks
    slots = last * LAG + 1

    early = chunks // 7 * LANES
    loads = []
    for k, cols in enumerate((pl.ds(0, early), pl.ds(early, chunks * LANES - early))):
        loads.append(
            pltpu.make_async_copy(unembed_ref.at[:, cols], weights.at[:, cols], w_sem.at[k])
        )
        loads[k].start()

    barrier = pltpu.get_barrier_semaphore()
    for k in range(1, n):
        pl.semaphore_signal(
            barrier, inc=1, device_id={"width": lax.rem(me + k, n)}, device_id_type=MESH
        )
    for k in range(1, nv):
        pl.semaphore_signal(
            barrier, inc=1, device_id={"vocab": lax.rem(my_vocab + k, nv)}, device_id_type=MESH
        )

    values = hidden_ref[...].astype(jnp.float32)
    square = jnp.mean(values * values, axis=1, keepdims=True)
    normed = (values * lax.rsqrt(square + 1e-05) * gain_ref[...][None, :]).astype(jnp.bfloat16)
    for j in range(n):
        blocks[j] = normed[:, j * share : (j + 1) * share]

    pl.semaphore_wait(barrier, n - 1 + nv - 1)

    my_part = pl.ds(pl.multiple_of(lax.rem(my_vocab, 2) * (own_rows // 2), own_rows // 2), own_rows // 2)
    other_part = pl.ds(
        pl.multiple_of((1 - lax.rem(my_vocab, 2)) * (own_rows // 2), own_rows // 2), own_rows // 2
    )
    partner = my_vocab + 1 - 2 * lax.rem(my_vocab, 2)

    def row_copy(peer, source):
        return pltpu.make_async_remote_copy(
            src_ref=blocks.at[peer, my_part],
            dst_ref=rows_in.at[source, my_part],
            send_sem=x_send.at[peer],
            recv_sem=x_recv.at[source],
            device_id={"width": peer},
            device_id_type=MESH,
        )

    def pass_rows(source, part):
        return pltpu.make_async_remote_copy(
            src_ref=rows_in.at[source, part],
            dst_ref=rows_in.at[source, part],
            send_sem=p_send.at[source],
            recv_sem=p_recv.at[source],
            device_id={"vocab": partner},
            device_id_type=MESH,
        )

    def send_rows():
        for k in range(1, n):
            row_copy(lax.rem(me + jnp.where(me < n // 2, k, n - k), n), me).start()

    rows_now = jnp.where(me < n // 2, me, last - me) < group_blocks

    @pl.when(rows_now)
    def _():
        send_rows()

    own = pltpu.make_async_copy(blocks.at[me], rows_in.at[me], own_sem)
    own.start()

    target_row = targets_ref[...].astype(jnp.float32)
    target_all = jnp.transpose(jnp.broadcast_to(target_row, (LANES, 2 * half)))
    target_cols[0] = target_all[:half]
    target_cols[1] = target_all[half:]
    state[0] = jnp.full((half, LANES), LOWEST, jnp.float32)
    for k in range(1, 4):
        state[k] = jnp.zeros((half, LANES), jnp.float32)

    own.wait()
    loads[0].wait()

    def chunk_copy(side, c, peer):
        return pltpu.make_async_remote_copy(
            src_ref=buf.at[side, c],
            dst_ref=buf.at[side, c],
            send_sem=c_send.at[side, lax.rem(c, slots)],
            recv_sem=c_recv.at[side, lax.rem(c, slots)],
            device_id={"width": peer},
            device_id_type=MESH,
        )

    first_col = my_vocab * (chunks * LANES)
    lane = lax.broadcasted_iota(jnp.int32, (half, LANES), 1)
    item_lane = lax.broadcasted_iota(jnp.int32, (group_rows, LANES), 1)

    def partial_logits(first_block, c):
        cols = pl.ds(pl.multiple_of(c * LANES, LANES), LANES)
        x = rows_in[pl.ds(first_block, group_blocks)].reshape(group_rows, share)
        return jnp.dot(x, weights[:, cols], preferred_element_type=jnp.float32)

    def take_stats(side, first_block, c, logits):
        rows = pl.ds(pl.multiple_of((first_block - side * (n // 2)) * own_rows, 8), group_rows)
        column = (first_col + c * LANES + item_lane).astype(jnp.float32)
        old_max = state[0, rows]
        new_max = jnp.maximum(old_max, logits)
        scale = jnp.exp(old_max - new_max)
        shifted = jnp.exp(logits - new_max)
        state[0, rows] = new_max
        state[1, rows] = state[1, rows] * scale + shifted
        state[2, rows] = state[2, rows] * scale + shifted * logits
        state[3, rows] = state[3, rows] + jnp.where(column == target_cols[side, rows], logits, 0.0)

    def advance(side, item, head, tail, peer):
        @pl.when((item >= 0) & (item < items))
        def _():
            group = item // chunks
            c = item - group * chunks
            first_block = group * group_blocks if side == 0 else n - (group + 1) * group_blocks
            for g in range(GROUPS):
                start = g * group_blocks if side == 0 else n - (g + 1) * group_blocks

                @pl.when(item == g * (chunks // 2))
                def _():
                    for w in range(start, start + group_blocks):

                        @pl.when(me != w)
                        def _():
                            row_copy(w, w).wait_recv()
                            pass_rows(w, my_part).start()

                @pl.when(item == g * chunks)
                def _():
                    for w in range(start, start + group_blocks):

                        @pl.when(me != w)
                        def _():
                            pass_rows(w, other_part).wait_recv()

            mine = partial_logits(first_block, c)

            @pl.when((me != tail) & (item >= slots))
            def _():
                chunk_copy(side, item - slots, peer).wait_send()

            @pl.when(me == head)
            def _():
                buf[side, item] = mine
                chunk_copy(side, item, peer).start()

            @pl.when(me != head)
            def _():
                chunk_copy(side, item, peer).wait_recv()
                total = buf[side, item] + mine

                @pl.when(me != tail)
                def _():
                    buf[side, item] = total
                    chunk_copy(side, item, peer).start()

                @pl.when(me == tail)
                def _():
                    take_stats(side, first_block, c, total)

    down = lax.rem(me + n - 1, n)
    up = lax.rem(me + 1, n)

    def step(s, carry):
        @pl.when(s == 1)
        def _():
            loads[1].wait()

        @pl.when((s == 2 * LAG) & jnp.logical_not(rows_now))
        def _():
            send_rows()

        advance(0, s - me * LAG, 0, last, up)
        advance(1, s - (last - me) * LAG, last, 0, down)
        return carry

    lax.fori_loop(0, items + last * LAG, step, 0)

    def stats_copy(peer, source):
        return pltpu.make_async_remote_copy(
            src_ref=packed.at[0],
            dst_ref=gathered.at[source],
            send_sem=v_send.at[peer],
            recv_sem=v_recv.at[source],
            device_id={"vocab": peer},
            device_id_type=MESH,
        )

    def final_copy(side, peer):
        return pltpu.make_async_remote_copy(
            src_ref=packed.at[1],
            dst_ref=final.at[side],
            send_sem=f_send.at[peer],
            recv_sem=f_recv.at[side],
            device_id={"width": peer},
            device_id_type=MESH,
        )

    def finish(side):
        lane_max = state[0]
        row_max = jnp.max(lane_max, axis=1, keepdims=True)
        scale = jnp.exp(lane_max - row_max)
        columns = (
            row_max,
            jnp.sum(state[1] * scale, axis=1, keepdims=True),
            jnp.sum(state[2] * scale, axis=1, keepdims=True),
            jnp.sum(state[3], axis=1, keepdims=True),
        )
        wide = jnp.zeros((half, LANES), jnp.float32)
        for k in range(4):
            wide = jnp.where(lane == k, columns[k], wide)
        flat = jnp.transpose(wide)[:8]
        packed[0] = flat
        for k in range(1, nv):
            stats_copy(lax.rem(my_vocab + k, nv), my_vocab).start()
        gathered[my_vocab] = flat
        for k in range(1, nv):
            peer = lax.rem(my_vocab + k, nv)
            stats_copy(peer, peer).wait_recv()
        parts = [gathered[v] for v in range(nv)]
        top = functools.reduce(jnp.maximum, [part[0:1] for part in parts])
        total = jnp.zeros_like(top)
        weighted = jnp.zeros_like(top)
        target = jnp.zeros_like(top)
        for part in parts:
            factor = jnp.exp(part[0:1] - top)
            total = total + part[1:2] * factor
            weighted = weighted + part[2:3] * factor
            target = target + part[3:4]
        log_normalizer = top + jnp.log(total)
        rows = lax.broadcasted_iota(jnp.int32, (8, half), 0)
        result = jnp.where(
            rows == 0,
            log_normalizer,
            jnp.where(rows == 1, log_normalizer - weighted / total, target - log_normalizer),
        )
        packed[1] = result
        for k in range(1, n):
            final_copy(side, lax.rem(me + k, n)).start()
        final[side] = result

    @pl.when(me == last)
    def _():
        finish(0)

    @pl.when(me == 0)
    def _():
        finish(1)

    @pl.when(me != last)
    def _():
        final_copy(0, 0).wait_recv()

    @pl.when(me != 0)
    def _():
        final_copy(1, 0).wait_recv()

    ids = lax.broadcasted_iota(jnp.int32, (LANES, half), 0)
    sums = jnp.zeros((LANES, 1), jnp.float32)
    counts = jnp.zeros((LANES, 1), jnp.float32)
    for side in range(2):
        member = ids == seq_ref[:, side * half : (side + 1) * half]
        sums = sums + jnp.sum(jnp.where(member, final[side, 2:3], 0.0), axis=1, keepdims=True)
        counts = counts + jnp.sum(member.astype(jnp.float32), axis=1, keepdims=True)
    means = sums / jnp.maximum(counts, 1.0)
    out_ref[...] = jnp.zeros_like(out_ref)
    out_ref[3:4, :] = jnp.transpose(jnp.broadcast_to(means, (LANES, LANES)))[0:1]
    for w in range(n):

        @pl.when(me == w)
        def _():
            start = (w % (n // 2)) * own_rows
            out_ref[0:3, 0:own_rows] = final[w // (n // 2), 0:3, start : start + own_rows]

    for k in range(1, n):
        row_copy(lax.rem(me + k, n), me).wait_send()
        pass_rows(lax.rem(me + k, n), my_part).wait_send()

    def drain(c, carry):
        @pl.when(me != last)
        def _():
            chunk_copy(0, c, up).wait_send()

        @pl.when(me != 0)
        def _():
            chunk_copy(1, c, down).wait_send()

        return carry

    lax.fori_loop(max(items - slots, 0), items, drain, 0)

    @pl.when((me == 0) | (me == last))
    def _():
        for k in range(1, nv):
            stats_copy(lax.rem(my_vocab + k, nv), my_vocab).wait_send()
        for k in range(1, n):
            final_copy(0, lax.rem(me + k, n)).wait_send()


def solution(mesh):
    n, nv = mesh.shape["width"], mesh.shape["vocab"]

    def local(hidden, gain, unembed, targets, seq_ids):
        own_rows, width_dim = hidden.shape
        share, columns = unembed.shape
        half = (n // 2) * own_rows
        items = GROUPS * (columns // LANES)
        vmem = pl.BlockSpec(memory_space=pltpu.VMEM)
        out = pl.pallas_call(
            functools.partial(kernel, n, nv),
            out_shape=jax.ShapeDtypeStruct((8, LANES), jnp.float32),
            in_specs=[vmem, vmem, pl.BlockSpec(memory_space=pl.ANY), vmem, vmem],
            out_specs=vmem,
            scratch_shapes=[
                pltpu.VMEM((share, columns), jnp.bfloat16),
                pltpu.VMEM((n, own_rows, share), jnp.bfloat16),
                pltpu.VMEM((n, own_rows, share), jnp.bfloat16),
                pltpu.VMEM((2, items, half // GROUPS, LANES), jnp.float32),
                pltpu.VMEM((2, half, LANES), jnp.float32),
                pltpu.VMEM((4, half, LANES), jnp.float32),
                pltpu.VMEM((2, 8, half), jnp.float32),
                pltpu.VMEM((nv, 8, half), jnp.float32),
                pltpu.VMEM((2, 8, half), jnp.float32),
                pltpu.SemaphoreType.DMA((2,)),
                pltpu.SemaphoreType.DMA,
                pltpu.SemaphoreType.DMA((n,)),
                pltpu.SemaphoreType.DMA((n,)),
                pltpu.SemaphoreType.DMA((n,)),
                pltpu.SemaphoreType.DMA((n,)),
                pltpu.SemaphoreType.DMA((2, (n - 1) * LAG + 1)),
                pltpu.SemaphoreType.DMA((2, (n - 1) * LAG + 1)),
                pltpu.SemaphoreType.DMA((nv,)),
                pltpu.SemaphoreType.DMA((nv,)),
                pltpu.SemaphoreType.DMA((n,)),
                pltpu.SemaphoreType.DMA((2,)),
            ],
            compiler_params=pltpu.CompilerParams(
                collective_id=0, has_side_effects=True, vmem_limit_bytes=66_000_000
            ),
        )(hidden, gain, unembed, targets[None, :], seq_ids[None, :])
        return out[0, :own_rows], out[1, :own_rows], out[2, :own_rows], out[3, :SEQS]

    return jax.shard_map(
        local,
        mesh=mesh,
        in_specs=(P("width", None), P(), P("width", "vocab"), P(), P()),
        out_specs=(P("width"), P("width"), P("width"), P()),
        check_vma=False,
    )
```
